32 devices in a mesh: dp: 32 (over z, y, x, core).
Axes of the slice: x: 2, y: 2, z: 4, core: 2. Of those that a mesh axis runs over, the one named last changes fastest.
Arguments:
- tokens: bfloat16 [32768, 768], P('dp'), may hold values from -6 to 6
- cotangent: bfloat16 [32768, 768], P('dp'), may hold values from -6 to 6
- cluster_order: int32 [32768], P('dp'), may hold values from 0 to 1023, as said below
- live_clusters: int32 [32], P('dp'), may hold values from 4 to 8, as said below
- step_count: int32 [1], replicated, may hold values from 1 to 20
- learn_rates: float32 [6], replicated, may hold values from 0.4 to 1
- w_qkv: float32 [768, 2304], P('dp'), may hold values from -0.21875 to 0.21875
- w_out: float32 [768, 768], P('dp'), may hold values from -2.5 to 2.5
- w_up: float32 [768, 3072], P('dp'), may hold values from -0.21875 to 0.21875
- w_down: float32 [3072, 768], P('dp'), may hold values from -0.109375 to 0.109375
- biases: float32 [7680], P('dp'), may hold values from -1.2 to 1.2
- norm_gains: float32 [1536], P('dp'), may hold values from 0.5 to 1.5
- m_qkv: float32 [768, 2304], P('dp'), may hold values from -0.00024414062 to 0.00024414062
- m_out: float32 [768, 768], P('dp'), may hold values from -4.5776367e-05 to 4.5776367e-05
- m_up: float32 [768, 3072], P('dp'), may hold values from -0.00012207031 to 0.00012207031
- m_down: float32 [3072, 768], P('dp'), may hold values from -0.00030517578 to 0.00030517578
- m_biases: float32 [7680], P('dp'), may hold values from -0.00030517578 to 0.00030517578
- m_gains: float32 [1536], P('dp'), may hold values from -0.00061035156 to 0.00061035156
- v_qkv: float32 [768, 2304], P('dp'), may hold values from 1.6349286e-10 to 6.5612266e-10
- v_out: float32 [768, 768], P('dp'), may hold values from 4.9865325e-12 to 1.994613e-11
- v_up: float32 [768, 3072], P('dp'), may hold values from 4.0873215e-11 to 1.6349286e-10
- v_down: float32 [3072, 768], P('dp'), may hold values from 2.544149e-10 to 1.0176596e-09
- v_biases: float32 [7680], P('dp'), may hold values from 2.544149e-10 to 1.0176596e-09
- v_gains: float32 [1536], P('dp'), may hold values from 1.0176596e-09 to 3.989226e-09
Outputs:
- output: bfloat16 [32768, 768], P('dp')
- input_grad: bfloat16 [32768, 768], P('dp')
- grad_norm: float32 [1], replicated
- new_m_qkv: float32 [768, 2304], P('dp')
- new_m_out: float32 [768, 768], P('dp')
- new_m_up: float32 [768, 3072], P('dp')
- new_m_down: float32 [3072, 768], P('dp')
- new_m_biases: float32 [7680], P('dp')
- new_m_gains: float32 [1536], P('dp')
- new_v_qkv: float32 [768, 2304], P('dp')
- new_v_out: float32 [768, 768], P('dp')
- new_v_up: float32 [768, 3072], P('dp')
- new_v_down: float32 [3072, 768], P('dp')
- new_v_biases: float32 [7680], P('dp')
- new_v_gains: float32 [1536], P('dp')
- new_w_qkv: float32 [768, 2304], P('dp')
- new_w_out: float32 [768, 768], P('dp')
- new_w_up: float32 [768, 3072], P('dp')
- new_w_down: float32 [3072, 768], P('dp')
- new_biases: float32 [7680], P('dp')
- new_gains: float32 [1536], P('dp')
The draws below stay inside these ranges and needn't reach their ends.
Inputs may be any that keep to these rules, and one draw needn't show every extreme that they name: `cluster_order`: on each device, a permutation of 0 to 1023. The device's items lie end to end from row 0, each 512 rows (short) or 1024 rows (long); the permutation keeps every item's rows inside the item and keeps dead rows among dead rows. The clusters of a device that hold item rows, a multiple of 4; its first live_clusters * 128 reordered rows are live. Some device holds 8.
All inputs are finite; a program needn't handle non-finite values.
Results may differ from the reference program's by a relative error of at most 0.015.
The reference program's roundings to bfloat16 on the way count: a program that leaves them out, or rounds other values in their place, can miss the bound.
Values may be sent and summed in bfloat16 or wider, within the bound.
No kernel may reach another device: no remote copies, remote signals or barrier semaphores. Data moves between devices by JAX's collectives and lax.ppermute only.
A program may use at most 256 MiB of HBM per device.

```python
import math
import jax
import jax.numpy as jnp
from jax import lax

D = 768
HEADS = 12
HEAD_DIM = 64
FF = 3072
CLUSTER = 128
SHORT_CL = 4
LONG_CL = 8
CAP = 1024
TOKENS = 32768


def deal_items(key):
    device_count = TOKENS // CAP
    ratio = LONG_CL // SHORT_CL
    device_kinds = jax.random.randint(jax.random.fold_in(key, 11), (device_count,), 0, ratio + 1)
    chosen = jax.random.randint(jax.random.fold_in(key, 12), (), 0, device_count)
    device_kinds = jnp.where(jnp.arange(device_count) == chosen, 0, device_kinds)
    live_count = jnp.where(device_kinds == 0, LONG_CL, device_kinds * SHORT_CL).astype(jnp.int32)
    item_rows = jnp.where(device_kinds == 0, CAP, SHORT_CL * CLUSTER).astype(jnp.int32)
    positions = jnp.arange(CAP, dtype=jnp.int32)
    device_keys = jax.random.split(jax.random.fold_in(key, 13), device_count)

    def one_device(device_key, live_here, rows_here):
        shuffle = jax.random.permutation(device_key, CAP).astype(jnp.int32)
        item_index = jnp.where(positions < live_here * CLUSTER, positions // rows_here, CAP)
        scores_int = item_index * CAP + shuffle
        return jnp.argsort(scores_int, stable=True).astype(jnp.int32)
    orders = jax.vmap(one_device)(device_keys, live_count, item_rows)
    return (orders.reshape(-1), live_count)


def draw_cluster_order(key, part):
    return deal_items(key)[0]


def draw_live_clusters(key, part):
    return deal_items(key)[1]


def strengthened(values, key, source, target, parts, factor):
    owner, partner = [(jnp.arange(values.shape[dim]) // (values.shape[dim] // parts)).reshape([-1 if axis == dim else 1 for axis in range(values.ndim)]) for dim in (source, target)]
    chosen = jax.random.permutation(key, parts)[partner]
    strong = (owner == chosen) | (owner == (partner + parts // 2) % parts)
    return jnp.where(strong, factor * values, values)


def block_scale(stream_key, dims, cuts, low, largest):
    gain, own = 1.0, jax.random.fold_in(stream_key, 6)
    for position, shards_of in cuts:
        heights = jnp.exp(jax.random.uniform(jax.random.fold_in(own, position), (shards_of,), jnp.float32, low / len(cuts), largest / len(cuts)))
        gain = gain * jnp.repeat(heights, dims[position] // shards_of).reshape([-1 if axis == position else 1 for axis in range(len(dims))])
    return gain


def normal_values(rng, shape, deviation, bound, shards=(), kind=jnp.bfloat16):
    array = jax.random.normal(rng, shape, jnp.float32) * deviation
    if len(shards) > 0:
        array = block_scale(rng, shape, shards, -0.22, 0.18) * array
    return jnp.clip(array, min=-bound, max=bound).astype(kind)


def noise_with(key, dims, width, most, cuts, heavy, kind=jnp.bfloat16):
    values = width * jax.random.normal(key, dims, jnp.float32)
    if cuts:
        values = values * block_scale(key, dims, cuts, -0.22, 0.18)
    return jnp.clip(strengthened(values, jax.random.fold_in(key, 3), *heavy), -most, most).astype(kind)


def setup_inputs(seed: int = 0) -> dict:
    arg_keys = jax.random.split(jax.random.key(seed), 25)
    return {
        "tokens": noise_with(arg_keys[0], (TOKENS, D), 1.0, 6.0, ((0, 32),), (0, 1, 32, 2.75)),
        "cotangent": normal_values(arg_keys[1], (TOKENS, D), 1.0, 6.0, ((0, 32),)),
        "cluster_order": draw_cluster_order(jax.random.fold_in(arg_keys[24], 71), 0),
        "live_clusters": draw_live_clusters(jax.random.fold_in(arg_keys[24], 71), 0),
        "step_count": jax.random.randint(arg_keys[4], (1,), 1, 21).astype(jnp.int32),
        "learn_rates": jnp.clip(jax.random.uniform(arg_keys[5], (6,), jnp.float32, 0.4, 1.0), 0.4, 1.0),
        "w_qkv": normal_values(arg_keys[6], (D, 3 * D), D ** -0.5, 0.21875, ((0, 32),), jnp.float32),
        "w_out": normal_values(arg_keys[7], (D, D), (D // CLUSTER) ** -0.5, 2.5, ((0, 32),), jnp.float32),
        "w_up": normal_values(arg_keys[8], (D, FF), D ** -0.5, 0.21875, ((0, 32),), jnp.float32),
        "w_down": normal_values(arg_keys[9], (FF, D), FF ** -0.5, 0.109375, ((0, 32),), jnp.float32),
        "biases": normal_values(arg_keys[10], (6 * D + FF,), 0.2, 1.2, ((0, 32),), jnp.float32),
        "norm_gains": jnp.clip(1.0 + 0.1 * jax.random.normal(arg_keys[11], (2 * D,), jnp.float32), 0.5, 1.5),
        "m_qkv": normal_values(arg_keys[12], (D, 3 * D), ((50 * (5 * D * D + 3 * D * FF)) ** -0.5), 0.00024414062, ((0, 32),), jnp.float32),
        "m_out": normal_values(arg_keys[13], (D, D), ((1600 * (5 * D * D + 3 * D * FF)) ** -0.5), 4.57763671875e-05, ((0, 32),), jnp.float32),
        "m_up": normal_values(arg_keys[14], (D, FF), ((200 * (5 * D * D + 3 * D * FF)) ** -0.5), 0.00012207031, ((0, 32),), jnp.float32),
        "m_down": normal_values(arg_keys[15], (FF, D), ((32 * (5 * D * D + 3 * D * FF)) ** -0.5), 0.00030517578, ((0, 32),), jnp.float32),
        "m_biases": normal_values(arg_keys[16], (6 * D + FF,), ((32 * (5 * D * D + 3 * D * FF)) ** -0.5), 0.00030517578, ((0, 32),), jnp.float32),
        "m_gains": normal_values(arg_keys[17], (2 * D,), ((8 * (5 * D * D + 3 * D * FF)) ** -0.5), 0.00061035156, ((0, 32),), jnp.float32),
        "v_qkv": jnp.clip(jnp.exp(math.log(6.561226562062927e-10) - 1.38957844 * jax.random.uniform(arg_keys[18], (D, 3 * D), jnp.float32) ** block_scale(arg_keys[18], (D, 3 * D), ((0, 32),), -0.2, 0.2)), 1.6349285814065695e-10, 6.561226562062927e-10),
        "v_out": jnp.clip(jnp.exp(math.log(1.994612981726096e-11) - 1.3862944 * jax.random.uniform(arg_keys[19], (D, D), jnp.float32) ** block_scale(arg_keys[19], (D, D), ((0, 32),), -0.2, 0.2)), 4.98653245431524e-12, 1.994612981726096e-11),
        "v_up": jnp.clip(jnp.exp(math.log(1.6349285814065695e-10) - 1.3862944 * jax.random.uniform(arg_keys[20], (D, FF), jnp.float32) ** block_scale(arg_keys[20], (D, FF), ((0, 32),), -0.2, 0.2)), 4.087321453516424e-11, 1.6349285814065695e-10),
        "v_down": jnp.clip(jnp.exp(math.log(1.0176596232369661e-09) - 1.3862944 * jax.random.uniform(arg_keys[21], (FF, D), jnp.float32) ** block_scale(arg_keys[21], (FF, D), ((0, 32),), -0.2, 0.2)), 2.5441490580924153e-10, 1.0176596232369661e-09),
        "v_biases": jnp.clip(jnp.exp(math.log(1.0176596232369661e-09) - 1.3862944 * jax.random.uniform(arg_keys[22], (6 * D + FF,), jnp.float32) ** block_scale(arg_keys[22], (6 * D + FF,), ((0, 32),), -0.2, 0.2)), 2.5441490580924153e-10, 1.0176596232369661e-09),
        "v_gains": jnp.clip(jnp.exp(math.log(3.989225838552102e-09) - 1.3660917 * jax.random.uniform(arg_keys[23], (2 * D,), jnp.float32) ** block_scale(arg_keys[23], (2 * D,), ((0, 32),), -0.2, 0.2)), 1.0176596232369661e-09, 3.989225838552102e-09),
    }


@jax.custom_vjp
def low(v):
    return lax.optimization_barrier(v.astype(jnp.bfloat16)).astype(jnp.float32)

@jax.custom_vjp
def low_back(v):
    return v

def low_keep(v):
    return (low(v), None)

def low_pass(kept, grad):
    return (grad,)

def back_keep(v):
    return (v, None)

def back_low(kept, grad):
    return (low(grad),)
low.defvjp(low_keep, low_pass)
low_back.defvjp(back_keep, back_low)
EPSILON = 1e-06
CLIP_BOUND = 1.0
BETA_ONE = 0.9
BETA_TWO = 0.999
ADAM_EPS = 1e-08
DECAY = 0.01
HIGHEST = lax.Precision.HIGHEST

def high_dot(left_side, right_side):
    return jnp.dot(left_side, right_side, precision=HIGHEST, preferred_element_type=jnp.float32)

def split_vectors(bias_all, gain_all):
    model_width = gain_all.shape[0] // 2
    hidden_width = bias_all.shape[0] - 6 * model_width
    bounds = (0, model_width, 2 * model_width, 3 * model_width, 3 * model_width + hidden_width, 4 * model_width + hidden_width, 5 * model_width + hidden_width, 6 * model_width + hidden_width)
    pieces = tuple((bias_all[bounds[number]:bounds[number + 1]] for number in range(7)))
    return pieces + (gain_all[:model_width], gain_all[model_width:])

def layer_norm(values, gain_vec, shift_vec):
    centred = values - lax.optimization_barrier(jnp.mean(values, axis=-1, keepdims=True))
    spread = lax.optimization_barrier(jnp.mean(centred * centred, axis=-1, keepdims=True))
    return centred * lax.rsqrt(spread + EPSILON) * gain_vec + shift_vec

def layer(params, ordered, live_mask):
    w_qkv, w_out, w_up, w_down, bias_all, gain_all = params
    b_query, b_value, b_out, b_up, b_down, shift_one, shift_two, gain_one, gain_two = split_vectors(bias_all, gain_all)
    row_count = ordered.shape[0]
    clusters_here = row_count // CLUSTER
    qkv_bias = jnp.concatenate([b_query, jnp.zeros_like(b_query), b_value])
    qkv_low = low(low_back(high_dot(ordered, w_qkv) + qkv_bias))
    shaped = qkv_low.reshape(clusters_here, CLUSTER, 3, HEADS, HEAD_DIM)
    query_low, key_low, value_low = (shaped[:, :, 0], shaped[:, :, 1], shaped[:, :, 2])
    raw = low_back(jnp.einsum('cqhe,ckhe->chqk', query_low, key_low, precision=HIGHEST))
    probs_full = jax.nn.softmax(raw * HEAD_DIM ** (-0.5), axis=-1)
    context = jnp.einsum('chqk,ckhe->cqhe', low(probs_full), value_low, precision=HIGHEST)
    context_low = low(low_back(context)).reshape(row_count, D)
    attn_out = low_back(high_dot(context_low, w_out) + b_out)
    first_sum = ordered + attn_out
    normed_one = layer_norm(first_sum, gain_one, shift_one)
    up_value = low_back(high_dot(low(normed_one), w_up) + b_up)
    hidden_low = low(jax.nn.gelu(up_value, approximate=False))
    ffn_out = low_back(high_dot(hidden_low, w_down) + b_down)
    second_sum = normed_one + ffn_out
    return layer_norm(second_sum, gain_two, shift_two) * live_mask[:, None]

def adam_update(masters, firsts, seconds, grads, grad_norm, step_count, learn_rates):
    factor = CLIP_BOUND / jnp.maximum(grad_norm, CLIP_BOUND)
    moment = step_count[0].astype(jnp.float32)
    first_fix = 1.0 - BETA_ONE ** moment
    second_fix = 1.0 - BETA_TWO ** moment
    base_rates = (D ** (-0.5), (D // CLUSTER) ** (-0.5), D ** (-0.5), FF ** (-0.5), 0.5, 0.5)
    new_firsts = []
    new_seconds = []
    new_masters = []
    for number in range(6):
        clipped = factor * grads[number]
        first_new = BETA_ONE * firsts[number] + (1.0 - BETA_ONE) * clipped
        second_new = BETA_TWO * seconds[number] + (1.0 - BETA_TWO) * clipped * clipped
        step_rate = learn_rates[number] * base_rates[number]
        update = first_new / first_fix / (jnp.sqrt(second_new / second_fix) + ADAM_EPS) + DECAY * masters[number]
        new_firsts.append(first_new)
        new_seconds.append(second_new)
        new_masters.append(masters[number] - step_rate * update)
    return (new_firsts, new_seconds, new_masters)

def reference(tokens, cotangent, cluster_order, live_clusters, step_count, learn_rates, w_qkv, w_out, w_up, w_down, biases, norm_gains, m_qkv, m_out, m_up, m_down, m_biases, m_gains, v_qkv, v_out, v_up, v_down, v_biases, v_gains):
    device_count = tokens.shape[0] // CAP
    orders = cluster_order.reshape(device_count, CAP).astype(jnp.int32)
    inverses = jnp.argsort(orders, axis=1).astype(jnp.int32)

    def arrange(values, index_table):
        shaped = values.reshape(device_count, CAP, -1)
        return jnp.take_along_axis(shaped, index_table[:, :, None], axis=1)
    ordered = arrange(tokens.astype(jnp.float32), orders)
    ordered_cot = arrange(cotangent.astype(jnp.float32), orders)
    positions = jnp.arange(CAP, dtype=jnp.int32)
    live_mask = (positions[None, :] < (live_clusters * CLUSTER)[:, None]).astype(jnp.float32)
    masters = (w_qkv, w_out, w_up, w_down, biases, norm_gains)

    def scan_step(running, inputs_triple):
        x_device, cot_device, mask_device = inputs_triple

        def forward(params, values):
            return layer(tuple((low(master) for master in params)), values, mask_device)
        result, pullback = jax.vjp(forward, masters, x_device)
        grads_here, input_here = pullback(cot_device)
        running = tuple((accumulated + addend for accumulated, addend in zip(running, grads_here)))
        return (running, (result, input_here))
    zero_grads = tuple((jnp.zeros_like(master) for master in masters))
    grads, stacked = lax.scan(scan_step, zero_grads, (ordered, ordered_cot, live_mask))
    results, input_grads = stacked
    output = arrange(results, inverses).reshape(tokens.shape).astype(jnp.bfloat16)
    input_grad = arrange(input_grads, inverses).reshape(tokens.shape).astype(jnp.bfloat16)
    squares = jnp.sum(jnp.stack([jnp.sum(grad_item * grad_item) for grad_item in grads]))
    grad_norm = jnp.sqrt(squares)
    firsts, seconds, updated = adam_update(masters, (m_qkv, m_out, m_up, m_down, m_biases, m_gains), (v_qkv, v_out, v_up, v_down, v_biases, v_gains), grads, grad_norm, step_count, learn_rates)
    return (output, input_grad, grad_norm.reshape(1), firsts[0], firsts[1], firsts[2], firsts[3], firsts[4], firsts[5], seconds[0], seconds[1], seconds[2], seconds[3], seconds[4], seconds[5], updated[0], updated[1], updated[2], updated[3], updated[4], updated[5])
```

```python
import functools

import jax
import jax.numpy as jnp
from jax import lax
from jax.experimental import pallas as pl
from jax.experimental.pallas import tpu as pltpu
from jax.sharding import PartitionSpec as P

HEAD_DIM = 64
CLUSTER = 128
PAIR = 2 * HEAD_DIM
ROWS = 256
BIAS_ROWS = 8

EPSILON = 1e-06
CLIP_BOUND = 1.0
BETA_ONE = 0.9
BETA_TWO = 0.999
ADAM_EPS = 1e-08
DECAY = 0.01
ROOT_HALF = 0.5**0.5
DENSITY = 0.3989422804014327

BF = jnp.bfloat16
F32 = jnp.float32
VMEM_LIMIT = 60 * 1024 * 1024


def dot(left, right):
    return lax.dot_general(left, right, (((1,), (0,)), ((), ())), preferred_element_type=F32)


def dot_nt(left, right):
    return lax.dot_general(left, right, (((1,), (1,)), ((), ())), preferred_element_type=F32)


def dot_tn(left, right):
    return lax.dot_general(left, right, (((0,), (0,)), ((), ())), preferred_element_type=F32)


def whole(shape):
    return pl.BlockSpec(shape, lambda *_: (0,) * len(shape))


def standardize(values):
    centred = values - jnp.mean(values, axis=-1, keepdims=True)
    spread = jnp.mean(centred * centred, axis=-1, keepdims=True)
    inverse = lax.rsqrt(spread + EPSILON)
    return centred * inverse, inverse


def norm_back(upstream, gain, xhat, inverse):
    scaled = upstream * gain
    mean_one = jnp.mean(scaled, axis=-1, keepdims=True)
    mean_two = jnp.mean(scaled * xhat, axis=-1, keepdims=True)
    return (scaled - mean_one - xhat * mean_two) * inverse


def column_sum(values):
    return jnp.sum(values, axis=0, keepdims=True)


def lane_masks(rows):
    lane = lax.broadcasted_iota(jnp.int32, (rows, PAIR), 1)
    return lane < HEAD_DIM


def stack_heads(block, low_half):
    zero = jnp.zeros_like(block)
    return jnp.concatenate(
        [jnp.where(low_half, block, zero), jnp.where(low_half, zero, block)], axis=0
    )


def pair_probs(query, key_stack):
    scaled = dot_nt(query, key_stack) * HEAD_DIM ** (-0.5)
    parts = []
    for half in range(2):
        part = scaled[:, half * CLUSTER : (half + 1) * CLUSTER]
        weight = jnp.exp(part - jnp.max(part, axis=-1, keepdims=True))
        parts.append(weight / jnp.sum(weight, axis=-1, keepdims=True))
    return parts


def attention_forward(qkv, context, rows, width):
    low_half = lane_masks(CLUSTER)
    for start in range(0, rows, CLUSTER):
        span = slice(start, start + CLUSTER)
        for col in range(0, width, PAIR):
            query = qkv[span, col : col + PAIR]
            keys = stack_heads(qkv[span, width + col : width + col + PAIR], low_half)
            vals = stack_heads(qkv[span, 2 * width + col : 2 * width + col + PAIR], low_half)
            probs = jnp.concatenate(pair_probs(query, keys), axis=1).astype(BF)
            context[span, col : col + PAIR] = dot(probs, vals).astype(BF)


def attention_backward(qkv, d_context, d_qkv, row, rows, width):
    low_half = lane_masks(CLUSTER)
    for start in range(0, rows, CLUSTER):
        span = slice(start, start + CLUSTER)
        out_span = pl.ds(pl.multiple_of(row + start, CLUSTER), CLUSTER)
        for col in range(0, width, PAIR):
            query = qkv[span, col : col + PAIR]
            keys = stack_heads(qkv[span, width + col : width + col + PAIR], low_half)
            vals = stack_heads(qkv[span, 2 * width + col : 2 * width + col + PAIR], low_half)
            d_ctx = d_context[span, col : col + PAIR]
            probs = pair_probs(query, keys)
            d_probs = dot_nt(d_ctx, vals)
            d_raw = []
            for half in range(2):
                part = d_probs[:, half * CLUSTER : (half + 1) * CLUSTER]
                mixed = probs[half] * part
                total = jnp.sum(mixed, axis=-1, keepdims=True)
                d_raw.append(((mixed - probs[half] * total) * HEAD_DIM ** (-0.5)).astype(BF))
            d_raw = jnp.concatenate(d_raw, axis=1)
            probs_low = jnp.concatenate(probs, axis=1).astype(BF)
            d_query = dot(d_raw, keys)
            d_key = dot_tn(d_raw, query)
            d_val = dot_tn(probs_low, d_ctx)
            d_key = jnp.where(low_half, d_key[:CLUSTER], d_key[CLUSTER:])
            d_val = jnp.where(low_half, d_val[:CLUSTER], d_val[CLUSTER:])
            d_qkv[out_span, col : col + PAIR] = d_query.astype(BF)
            d_qkv[out_span, width + col : width + col + PAIR] = d_key.astype(BF)
            d_qkv[out_span, 2 * width + col : 2 * width + col + PAIR] = d_val.astype(BF)


def attn_forward_kernel(width, x_ref, w_ref, vec_ref, gain_ref, qkv_ref, ctx_ref, xhat_ref, inv_ref):
    x_low = x_ref[...]
    for part in range(3):
        value = dot(x_low, w_ref[part])
        if part != 1:
            offset = 0 if part == 0 else width
            value = value + vec_ref[:, offset : offset + width]
        qkv_ref[:, part * width : (part + 1) * width] = value.astype(BF)
    attention_forward(qkv_ref, ctx_ref, x_ref.shape[0], width)
    attn = dot(ctx_ref[...], w_ref[3]) + vec_ref[:, 2 * width : 3 * width]
    xhat, inverse = standardize(x_low.astype(F32) + attn)
    xhat_ref[...] = xhat
    inv_ref[...] = jnp.broadcast_to(inverse, inv_ref.shape)


def attn_forward(x, w_attn, vectors, gains):
    rows, width = x.shape
    row_spec = lambda cols: pl.BlockSpec((ROWS, cols), lambda i: (i, 0))
    return pl.pallas_call(
        functools.partial(attn_forward_kernel, width),
        grid=(rows // ROWS,),
        in_specs=[row_spec(width), whole(w_attn.shape), whole(vectors.shape), whole(gains.shape)],
        out_specs=[row_spec(3 * width), row_spec(width), row_spec(width), row_spec(128)],
        out_shape=[
            jax.ShapeDtypeStruct((rows, 3 * width), BF),
            jax.ShapeDtypeStruct((rows, width), BF),
            jax.ShapeDtypeStruct((rows, width), F32),
            jax.ShapeDtypeStruct((rows, 128), F32),
        ],
        compiler_params=pltpu.CompilerParams(vmem_limit_bytes=VMEM_LIMIT),
        cost_estimate=pl.CostEstimate(
            flops=8 * rows * width * width, bytes_accessed=24 * rows * width, transcendentals=0
        ),
        name="attn_forward",
    )(x, w_attn, vectors, gains)


def ffn_forward_kernel(
    width, hidden_width, live_ref, xhat_ref, c_ref, up_w, down_w, vec_ref, gain_ref,
    hid_ref, slope_ref, out_ref, dsec_ref, sums_ref, low, acc,
):
    step = pl.program_id(0)
    rows = xhat_ref.shape[0]
    chunk = up_w.shape[1]
    shift_at = 4 * width + hidden_width

    def normed_rows(span):
        return xhat_ref[span, :] * gain_ref[:, :width] + vec_ref[:, shift_at : shift_at + width]

    @pl.when(step == 0)
    def _():
        for start in range(0, rows, ROWS):
            span = slice(start, start + ROWS)
            value = normed_rows(span)
            low[span, :] = value.astype(BF)
            acc[span, :] = value + vec_ref[:, 3 * width + hidden_width : shift_at]

    b_up = vec_ref[:, pl.ds(pl.multiple_of(3 * width + step * chunk, 128), chunk)]
    for start in range(0, rows, ROWS):
        span = slice(start, start + ROWS)
        up = dot(low[span, :], up_w[...]) + b_up
        phi = 0.5 + 0.5 * lax.erf(up * ROOT_HALF)
        slope_ref[span, :] = (phi + up * (jnp.exp(-0.5 * up * up) * DENSITY)).astype(BF)
        hidden = (up * phi).astype(BF)
        hid_ref[span, :] = hidden
        acc[span, :] += dot(hidden, down_w[...])

    @pl.when(step == pl.num_programs(0) - 1)
    def _():
        live_rows = live_ref[0] * CLUSTER
        gain = gain_ref[:, width:]
        shift = vec_ref[:, shift_at + width :]
        sums = [jnp.zeros((1, width), F32) for _ in range(3)]
        for start in range(0, rows, ROWS):
            span = slice(start, start + ROWS)
            xhat, inverse = standardize(acc[span, :])
            live = lax.broadcasted_iota(jnp.int32, (ROWS, width), 0) + start < live_rows
            out_ref[span, :] = jnp.where(live, xhat * gain + shift, 0.0).astype(BF)
            c = jnp.where(live, c_ref[span, :].astype(F32), 0.0)
            d_second = norm_back(c, gain, xhat, inverse)
            dsec_ref[span, :] = d_second
            sums[0] += column_sum(d_second.astype(BF).astype(F32))
            sums[1] += column_sum(c)
            sums[2] += column_sum(c * xhat)
        sums_ref[...] = jnp.concatenate(sums + [jnp.zeros((5, width), F32)], axis=0)


def ffn_forward(live, xhat, c, w_up, w_down, vectors, gains):
    rows, width = xhat.shape
    steps = w_up.shape[0]
    hidden_width = steps * width
    chunk_out = pl.BlockSpec((rows, width), lambda i, _: (0, i))
    weight = pl.BlockSpec((None, width, width), lambda i, _: (i, 0, 0))
    return pl.pallas_call(
        functools.partial(ffn_forward_kernel, width, hidden_width),
        grid_spec=pltpu.PrefetchScalarGridSpec(
            num_scalar_prefetch=1,
            grid=(steps,),
            in_specs=[
                whole(xhat.shape), whole(c.shape), weight, weight,
                whole(vectors.shape), whole(gains.shape),
            ],
            out_specs=[
                chunk_out, chunk_out, whole((rows, width)), whole((rows, width)), whole((8, width)),
            ],
            scratch_shapes=[pltpu.VMEM((rows, width), BF), pltpu.VMEM((rows, width), F32)],
        ),
        out_shape=[
            jax.ShapeDtypeStruct((rows, hidden_width), BF),
            jax.ShapeDtypeStruct((rows, hidden_width), BF),
            jax.ShapeDtypeStruct((rows, width), BF),
            jax.ShapeDtypeStruct((rows, width), F32),
            jax.ShapeDtypeStruct((8, width), F32),
        ],
        compiler_params=pltpu.CompilerParams(vmem_limit_bytes=VMEM_LIMIT),
        cost_estimate=pl.CostEstimate(
            flops=4 * rows * width * hidden_width, bytes_accessed=40 * rows * width, transcendentals=0
        ),
        name="ffn_forward",
    )(live, xhat, c, w_up, w_down, vectors, gains)


def ffn_backward_kernel(
    width, hidden_width, dsec_ref, hid_ref, slope_ref, up_w, down_w, xhat_ref, inv_ref, vec_ref, gain_ref,
    gup_ref, gdown_ref, bup_ref, dfirst_ref, sums_ref, d_ffn, low, acc, d_up,
):
    step = pl.program_id(0)
    rows = xhat_ref.shape[0]
    shift_at = 4 * width + hidden_width

    @pl.when(step == 0)
    def _():
        for start in range(0, rows, ROWS):
            span = slice(start, start + ROWS)
            d_ffn[span, :] = dsec_ref[span, :].astype(BF)
            acc[span, :] = dsec_ref[span, :]
            normed = xhat_ref[span, :] * gain_ref[:, :width] + vec_ref[:, shift_at : shift_at + width]
            low[span, :] = normed.astype(BF)

    total = jnp.zeros((1, width), F32)
    for start in range(0, rows, ROWS):
        span = slice(start, start + ROWS)
        value = (dot_nt(d_ffn[span, :], down_w[...]) * slope_ref[span, :].astype(F32)).astype(BF)
        d_up[span, :] = value
        total += column_sum(value.astype(F32))
        acc[span, :] += dot_nt(value, up_w[...])
    bup_ref[...] = jnp.broadcast_to(total, bup_ref.shape)
    for start in range(0, width, ROWS):
        span = slice(start, start + ROWS)
        gdown_ref[span, :] = dot_tn(hid_ref[:, span], d_ffn[...]).astype(BF)
        gup_ref[span, :] = dot_tn(low[:, span], d_up[...]).astype(BF)

    @pl.when(step == pl.num_programs(0) - 1)
    def _():
        gain = gain_ref[:, :width]
        sums = [jnp.zeros((1, width), F32) for _ in range(3)]
        for start in range(0, rows, ROWS):
            span = slice(start, start + ROWS)
            d_normed = acc[span, :]
            xhat = xhat_ref[span, :]
            d_first = norm_back(d_normed, gain, xhat, inv_ref[span, :1])
            dfirst_ref[span, :] = d_first
            sums[0] += column_sum(d_first.astype(BF).astype(F32))
            sums[1] += column_sum(d_normed)
            sums[2] += column_sum(d_normed * xhat)
        sums_ref[...] = jnp.concatenate(sums + [jnp.zeros((5, width), F32)], axis=0)


def ffn_backward(d_second, hidden, slope, w_up, w_down, xhat, inverse, vectors, gains):
    rows, width = xhat.shape
    steps = w_up.shape[0]
    hidden_width = steps * width
    chunk = pl.BlockSpec((rows, width), lambda i: (0, i))
    weight = pl.BlockSpec((None, width, width), lambda i: (i, 0, 0))
    return pl.pallas_call(
        functools.partial(ffn_backward_kernel, width, hidden_width),
        grid=(steps,),
        in_specs=[
            whole(d_second.shape), chunk, chunk, weight, weight, whole(xhat.shape), whole(inverse.shape),
            whole(vectors.shape), whole(gains.shape),
        ],
        out_specs=[
            weight, weight, pl.BlockSpec((8, width), lambda i: (0, i)),
            whole((rows, width)), whole((8, width)),
        ],
        scratch_shapes=[
            pltpu.VMEM((rows, width), BF), pltpu.VMEM((rows, width), BF),
            pltpu.VMEM((rows, width), F32), pltpu.VMEM((rows, width), BF),
        ],
        out_shape=[
            jax.ShapeDtypeStruct((steps, width, width), BF),
            jax.ShapeDtypeStruct((steps, width, width), BF),
            jax.ShapeDtypeStruct((8, hidden_width), F32),
            jax.ShapeDtypeStruct((rows, width), F32),
            jax.ShapeDtypeStruct((8, width), F32),
        ],
        compiler_params=pltpu.CompilerParams(vmem_limit_bytes=VMEM_LIMIT),
        cost_estimate=pl.CostEstimate(
            flops=8 * rows * width * hidden_width, bytes_accessed=60 * rows * width, transcendentals=0
        ),
        name="ffn_backward",
    )(d_second, hidden, slope, w_up, w_down, xhat, inverse, vectors, gains)


def attn_backward_kernel(
    width, dfirst_ref, ctx_ref, qkv_ref, x_ref, w_ref, dx_ref, grad_ref, sums_ref,
    d_attn, d_ctx, d_qkv, x_all, ctx_all, totals,
):
    step = pl.program_id(0)
    block = x_ref.shape[0]
    row = pl.multiple_of(step * block, block)
    span = pl.ds(row, block)

    @pl.when(step == 0)
    def _():
        totals[...] = jnp.zeros_like(totals)

    d_low = dfirst_ref[...].astype(BF)
    d_attn[span, :] = d_low
    x_all[span, :] = x_ref[...]
    ctx_all[span, :] = ctx_ref[...]
    d_ctx[...] = dot_nt(d_low, w_ref[3]).astype(BF)
    attention_backward(qkv_ref, d_ctx, d_qkv, row, block, width)
    value = dfirst_ref[...]
    for part in range(3):
        piece = d_qkv[span, part * width : (part + 1) * width]
        value = value + dot_nt(piece, w_ref[part])
        totals[part : part + 1, :] += column_sum(piece.astype(F32))
    dx_ref[...] = value.astype(BF)

    @pl.when(step == pl.num_programs(0) - 1)
    def _():
        for start in range(0, width, ROWS):
            piece = slice(start, start + ROWS)
            for part in range(3):
                cols = slice(part * width, (part + 1) * width)
                grad_ref[part, piece, :] = dot_tn(x_all[:, piece], d_qkv[:, cols]).astype(BF)
            grad_ref[3, piece, :] = dot_tn(ctx_all[:, piece], d_attn[...]).astype(BF)
        sums_ref[...] = totals[...]


def attn_backward(d_first, context, qkv, x, w_attn):
    rows, width = x.shape
    row_spec = lambda cols: pl.BlockSpec((ROWS, cols), lambda i: (i, 0))
    return pl.pallas_call(
        functools.partial(attn_backward_kernel, width),
        grid=(rows // ROWS,),
        in_specs=[row_spec(width), row_spec(width), row_spec(3 * width), row_spec(width), whole(w_attn.shape)],
        out_specs=[row_spec(width), whole(w_attn.shape), whole((8, width))],
        scratch_shapes=[
            pltpu.VMEM((rows, width), BF), pltpu.VMEM((ROWS, width), BF),
            pltpu.VMEM((rows, 3 * width), BF), pltpu.VMEM((rows, width), BF),
            pltpu.VMEM((rows, width), BF), pltpu.VMEM((8, width), F32),
        ],
        out_shape=[
            jax.ShapeDtypeStruct((rows, width), BF),
            jax.ShapeDtypeStruct(w_attn.shape, BF),
            jax.ShapeDtypeStruct((8, width), F32),
        ],
        compiler_params=pltpu.CompilerParams(vmem_limit_bytes=VMEM_LIMIT),
        cost_estimate=pl.CostEstimate(
            flops=16 * rows * width * width, bytes_accessed=24 * rows * width, transcendentals=0
        ),
        name="attn_backward",
    )(d_first, context, qkv, x, w_attn)


def digits_of(count):
    return {32: (2, 2, 2, 4), 256: (2, 8, 4, 4)}.get(count, (count,))


def total_over(value, count):
    stride = 1
    for radix in digits_of(count):
        parts = [value]
        for offset in range(1, radix):
            perm = [(d, partner(d, stride, radix, offset)) for d in range(count)]
            parts.append(lax.ppermute(value, "dp", perm))
        if radix & (radix - 1) == 0:
            while len(parts) > 1:
                parts = [parts[i] + parts[i + 1] for i in range(0, len(parts), 2)]
        value = parts[0]
        stride *= radix
    return value


def partner(device, stride, radix, offset):
    digit = device // stride % radix
    return device + ((digit ^ offset) - digit) * stride


def to_blocks(matrix, width):
    return [matrix[:, start : start + width] for start in range(0, matrix.shape[1], width)]


def adam_update(masters, firsts, seconds, grads, grad_norm, step_count, learn_rates, base_rates):
    factor = CLIP_BOUND / jnp.maximum(grad_norm, CLIP_BOUND)
    moment = step_count[0].astype(F32)
    first_fix = 1.0 - BETA_ONE**moment
    second_fix = 1.0 - BETA_TWO**moment
    new_firsts, new_seconds, new_masters = [], [], []
    for number in range(6):
        clipped = factor * grads[number]
        first_new = BETA_ONE * firsts[number] + (1.0 - BETA_ONE) * clipped
        second_new = BETA_TWO * seconds[number] + (1.0 - BETA_TWO) * clipped * clipped
        step_rate = learn_rates[number] * base_rates[number]
        update = (
            first_new / first_fix / (jnp.sqrt(second_new / second_fix) + ADAM_EPS)
            + DECAY * masters[number]
        )
        new_firsts.append(first_new)
        new_seconds.append(second_new)
        new_masters.append(masters[number] - step_rate * update)
    return new_firsts, new_seconds, new_masters


def body(count, tokens, cotangent, cluster_order, live_clusters, step_count, learn_rates, *state):
    masters, moments_one, moments_two = state[:6], state[6:12], state[12:]
    w_qkv, w_out, w_up, w_down, biases, norm_gains = (value.astype(BF) for value in masters)
    rows, width = tokens.shape
    local = w_qkv.shape[0]
    local_down = w_down.shape[0]
    chunks = w_up.shape[1] // width
    hidden_width = chunks * width
    small = jnp.pad(
        jnp.concatenate([biases, norm_gains]),
        (0, BIAS_ROWS * width - biases.shape[0] - norm_gains.shape[0]),
    ).reshape(BIAS_ROWS, width)
    shard = jnp.concatenate(
        to_blocks(w_qkv, width) + [w_out] + to_blocks(w_up, width) + [w_down, small], axis=0
    )
    gathered = lax.all_gather(shard, "dp", axis=0, tiled=True).reshape(count, shard.shape[0], width)
    attn_rows, up_rows = 4 * local, (4 + chunks) * local
    w_attn = gathered[:, :attn_rows].reshape(count, 4, local, width)
    w_attn = w_attn.transpose(1, 0, 2, 3).reshape(4, width, width)
    up_all = gathered[:, attn_rows:up_rows].reshape(count, chunks, local, width)
    up_all = up_all.transpose(1, 0, 2, 3).reshape(chunks, width, width)
    down_all = gathered[:, up_rows : up_rows + local_down].reshape(chunks, width, width)
    small_all = gathered[:, up_rows + local_down :].reshape(count, BIAS_ROWS * width).astype(F32)
    vectors = small_all[:, : biases.shape[0]].reshape(1, -1)
    gains = small_all[:, biases.shape[0] : biases.shape[0] + norm_gains.shape[0]].reshape(1, -1)

    position = jnp.arange(rows, dtype=jnp.int32)
    select = (cluster_order[:, None] == position[None, :]).astype(BF)
    restore = (cluster_order[None, :] == position[:, None]).astype(BF)
    x = dot(select, tokens).astype(BF)
    c = dot(select, cotangent).astype(BF)

    qkv, context, xhat, inverse = attn_forward(x, w_attn, vectors, gains)
    hidden, slope, out_rows, d_second, sums_two = ffn_forward(
        live_clusters, xhat, c, up_all, down_all, vectors, gains
    )
    g_up, g_down, g_bup, d_first, sums_one = ffn_backward(
        d_second, hidden, slope, up_all, down_all, xhat, inverse, vectors, gains
    )
    ffn_bucket = jnp.concatenate(
        [
            g_up.reshape(chunks, count, local, width).transpose(1, 0, 2, 3).reshape(count, -1, width),
            g_down.reshape(count, local_down, width),
        ],
        axis=1,
    )
    ffn_grad = lax.psum_scatter(
        ffn_bucket.reshape(-1, width), "dp", scatter_dimension=0, tiled=True
    ).astype(F32)
    dx_rows, g_attn, sums_qkv = attn_backward(d_first, context, qkv, x, w_attn)
    g_bias = jnp.concatenate(
        [sums_qkv[0], sums_qkv[2], sums_one[0], g_bup[0], sums_two[0], sums_one[1], sums_two[1]]
    ).reshape(count, -1)
    g_gain = jnp.concatenate([sums_one[2], sums_two[2]]).reshape(count, -1)
    g_small = jnp.concatenate([g_bias, g_gain], axis=1)
    g_small = jnp.pad(g_small, ((0, 0), (0, BIAS_ROWS * width - g_small.shape[1])))
    attn_bucket = jnp.concatenate(
        [
            g_attn.reshape(4, count, local, width).transpose(1, 0, 2, 3).reshape(count, -1, width),
            g_small.astype(BF).reshape(count, BIAS_ROWS, width),
        ],
        axis=1,
    )
    attn_grad = lax.psum_scatter(
        attn_bucket.reshape(-1, width), "dp", scatter_dimension=0, tiled=True
    ).astype(F32)
    output = dot(restore, out_rows).astype(BF)
    input_grad = dot(restore, dx_rows).astype(BF)
    square = jnp.sum(ffn_grad * ffn_grad) + jnp.sum(attn_grad * attn_grad)
    grad_norm = jnp.sqrt(total_over(jnp.full((8, 128), square, F32), count)[0, 0])
    small_grad = attn_grad[attn_rows:].reshape(-1)
    reduced = (
        jnp.concatenate([attn_grad[part * local : (part + 1) * local] for part in range(3)], axis=1),
        attn_grad[3 * local : attn_rows],
        jnp.concatenate([ffn_grad[k * local : (k + 1) * local] for k in range(chunks)], axis=1),
        ffn_grad[chunks * local :],
        small_grad[: biases.shape[0]],
        small_grad[biases.shape[0] : biases.shape[0] + norm_gains.shape[0]],
    )
    base_rates = (width**-0.5, (width // CLUSTER) ** -0.5, width**-0.5, hidden_width**-0.5, 0.5, 0.5)
    firsts, seconds, updated = adam_update(
        masters, moments_one, moments_two, reduced, grad_norm, step_count, learn_rates, base_rates
    )
    return (output, input_grad, grad_norm.reshape(1), *firsts, *seconds, *updated)


def solution(mesh):
    state = (P("dp", None),) * 4 + (P("dp"),) * 2
    return jax.shard_map(
        functools.partial(body, mesh.size),
        mesh=mesh,
        in_specs=(P("dp", None), P("dp", None), P("dp"), P("dp"), P(), P()) + state * 3,
        out_specs=(P("dp", None), P("dp", None), P()) + state * 3,
        check_vma=False,
    )
```
